32 devices in a mesh: grp: 2 (over y), gx: 16 (over z, x, core).
Axes of the slice: x: 2, y: 2, z: 4, core: 2. Of those that a mesh axis runs over, the one named last changes fastest.
Arguments:
- activations: bfloat16 [4, 32, 64, 4, 1024], P('grp', None, 'gx'), parts along dimension 0, may hold values from -6 to 6
- cotangent: bfloat16 [4, 32, 64, 4, 1024], P('grp', None, 'gx'), parts along dimension 0, may hold values from -6 to 6
- kernel: bfloat16 [32, 32, 3, 3, 3], replicated, may hold values from -0.21875 to 0.21875
- channel_bias: float32 [32], replicated, may hold values from -3 to 3
Outputs:
- activated: bfloat16 [4, 32, 64, 4, 1024], P('grp', None, 'gx'), parts along dimension 0
- grad_input: bfloat16 [4, 32, 64, 4, 1024], P('grp', None, 'gx'), parts along dimension 0
- grad_kernel: float32 [64, 32, 3, 3, 3], P('grp'), parts along dimension 0
- grad_bias: float32 [64], P('grp'), parts along dimension 0
The draws below stay inside these ranges and needn't reach their ends.
There are 2 independent parts, one for each index of `grp`. The reference program is written for one: setup_inputs(seed, part) draws one part's arguments, and reference() takes and returns one part's arrays. A program takes and returns all parts, laid end to end along the dimension named above; an argument that names none is the same for every part. Nothing has to cross between parts.
All inputs are finite; a program needn't handle non-finite values.
Results may differ from the reference program's by a relative error of at most 0.0055.
Values may be sent and summed in bfloat16 or wider, within the bound.
A program may use at most 256 MiB of HBM per device.

```python
import jax
import jax.numpy as jnp
from jax import lax

C = 32
B = 2
YB = 4
Z = 1024
NX = 64


def block_scale(own_key, extent, pieces, low, top_value):
    def one(axis_at, parts):
        steps = jax.random.uniform(jax.random.fold_in(jax.random.fold_in(own_key, 6), axis_at), (parts,), jnp.float32, low / len(pieces), top_value / len(pieces))
        return jnp.repeat(jnp.exp(steps), extent[axis_at] // parts).reshape((-1,) + (1,) * (len(extent) - axis_at - 1))

    loudness = one(*pieces[0])
    for cut in pieces[1:]:
        loudness = loudness * one(*cut)
    return loudness


def scatter_about(rng, dims, scale, most, split=(), kind=jnp.bfloat16):
    drawn = scale * jax.random.normal(rng, dims, jnp.float32)
    if split:
        drawn = drawn * block_scale(rng, dims, split, -0.22, 0.18)
    return jnp.clip(drawn, -most, most).astype(kind)


def setup_inputs(seed: int = 0, part: int = 0) -> dict:
    splits = jax.random.split(jax.random.key(seed), 5)
    own_keys = jax.random.split(jax.random.fold_in(splits[4], part), 5)
    return {
        "activations": scatter_about(own_keys[0], (B, C, NX, YB, Z), 1.0, 6.0, ((2, 16),)),
        "cotangent": scatter_about(own_keys[1], (B, C, NX, YB, Z), 1.0, 6.0, ((2, 16),)),
        "kernel": scatter_about(splits[2], (C, C, 3, 3, 3), (27 * C) ** -0.5, 0.21875),
        "channel_bias": scatter_about(splits[3], (C,), 0.5, 3.0, (), jnp.float32),
    }


def convolve(source, filters, xpad):
    return lax.conv_general_dilated(source, filters, (1, 1, 1), ((xpad, xpad), (1, 1), (1, 1)), dimension_numbers=("NCDHW", "OIDHW", "NCDHW"), preferred_element_type=jnp.float32)


def gelu_parts(before):
    cumulative = 0.5 * (1.0 + lax.erf(before * 0.7071067811865476))
    density = jnp.exp(-0.5 * before * before) * 0.3989422804014327
    return before * cumulative, cumulative + before * density


def reference(activations, cotangent, kernel, channel_bias):
    before = convolve(activations, kernel, 1) + channel_bias.astype(jnp.float32)[None, :, None, None, None]
    activated_full, derivative = gelu_parts(before)
    activated = activated_full.astype(jnp.bfloat16)
    delta = (cotangent.astype(jnp.float32) * derivative).astype(jnp.bfloat16)
    flipped = jnp.transpose(kernel[:, :, ::-1, ::-1, ::-1], (1, 0, 2, 3, 4))
    grad_input = convolve(delta, flipped, 1).astype(jnp.bfloat16)
    normalizer = float(B * NX * YB * Z) ** -0.5
    padded = jnp.pad(activations, ((0, 0), (0, 0), (1, 1), (1, 1), (1, 1))).astype(jnp.float32)
    delta_wide = delta.astype(jnp.float32)
    nx_cells = delta.shape[2]
    rows = []
    for offset_i in range(3):
        for offset_j in range(3):
            for offset_k in range(3):
                window = padded[:, :, offset_i:offset_i + nx_cells, offset_j:offset_j + YB, offset_k:offset_k + Z]
                rows.append(jnp.einsum("bcxyz,boxyz->oc", window, delta_wide))
    stacked = jnp.stack(rows, axis=-1).reshape(C, C, 3, 3, 3)
    grad_kernel = stacked * normalizer
    grad_bias = jnp.sum(delta_wide, axis=(0, 2, 3, 4)) * normalizer
    return activated, grad_input, grad_kernel, grad_bias
```

```python
import functools

import jax
import jax.numpy as jnp
from jax import lax
from jax.experimental import pallas as pl
from jax.experimental.pallas import tpu as pltpu
from jax.sharding import PartitionSpec as P

F32 = jnp.float32
BF16 = jnp.bfloat16


def one_hot_rows(rows, group, dtype):
    r = lax.broadcasted_iota(jnp.int32, (rows, rows // group), 0)
    c = lax.broadcasted_iota(jnp.int32, (rows, rows // group), 1)
    return jnp.where(r // group == c, 1.0, 0.0).astype(dtype)


def one_hot_cols(rows, group, dtype):
    r = lax.broadcasted_iota(jnp.int32, (rows // group, rows), 0)
    c = lax.broadcasted_iota(jnp.int32, (rows // group, rows), 1)
    return jnp.where(c // group == r, 1.0, 0.0).astype(dtype)


def band(rows, yb):
    r = lax.broadcasted_iota(jnp.int32, (rows, rows), 0)
    c = lax.broadcasted_iota(jnp.int32, (rows, rows), 1)
    return c % yb - r % yb


def build_weights(taps_ref, w_ref, rows, yb, backward):
    spread_rows = one_hot_rows(rows, yb, BF16)
    spread_cols = one_hot_cols(rows, yb, BF16)
    offset = band(rows, yb)
    w_ref[...] = jnp.zeros_like(w_ref)
    for i in range(3):
        for k in range(3):
            block = jnp.zeros((rows, rows), F32)
            for j in range(3):
                tap = taps_ref[(i * 3 + j) * 3 + k]
                wide = jnp.dot(tap, spread_cols, preferred_element_type=F32).astype(BF16)
                full = jnp.dot(spread_rows, wide, preferred_element_type=F32)
                want = (1 - j) if backward else (j - 1)
                block = block + jnp.where(offset == want, full, 0.0)
            block = block.astype(BF16)
            for xo in range(2):
                xi = xo - i + 2 if backward else xo + i
                w_ref[k, xo * rows:(xo + 1) * rows, xi * rows:(xi + 1) * rows] = block


def shifted(v):
    zero = jnp.zeros((v.shape[0], 1), v.dtype)
    return (
        jnp.concatenate([zero, v[:, :-1]], axis=1),
        jnp.concatenate([v[:, 1:], zero], axis=1),
    )


def forward_kernel(act_ref, lo_ref, hi_ref, cot_ref, taps_ref, bias_ref,
                   activated_ref, delta_ref, planes_ref, w_ref, s_ref):
    _, c, nx, yb, z = act_ref.shape
    rows = c * yb

    @pl.when(pl.program_id(0) == 0)
    def _():
        build_weights(taps_ref, w_ref, rows, yb, False)

    for p in range(nx + 2):
        if p == 0:
            v = lo_ref[0, :, 0]
        elif p == nx + 1:
            v = hi_ref[0, :, 0]
        else:
            v = act_ref[0, :, p - 1]
        v = v.reshape(rows, z)
        planes_ref[0, p] = v
        before, after = shifted(v)
        at = slice(p * rows, (p + 1) * rows)
        s_ref[0, at] = before
        s_ref[1, at] = v
        s_ref[2, at] = after
    zc = 256
    for q in range(nx // 2):
        at = slice(2 * q * rows, (2 * q + 4) * rows)
        for n in range(z // zc):
            zs = slice(n * zc, (n + 1) * zc)
            pre = jnp.dot(w_ref[0], s_ref[0, at, zs], preferred_element_type=F32)
            pre += jnp.dot(w_ref[1], s_ref[1, at, zs], preferred_element_type=F32)
            pre += jnp.dot(w_ref[2], s_ref[2, at, zs], preferred_element_type=F32)
            for xo in range(2):
                x = 2 * q + xo
                t = pre[xo * rows:(xo + 1) * rows] + bias_ref[:, 0:1]
                cumulative = 0.5 * (1.0 + lax.erf(t * 0.7071067811865476))
                density = jnp.exp(-0.5 * t * t) * 0.3989422804014327
                activated_ref[0, :, x, :, zs] = (t * cumulative).astype(BF16).reshape(c, yb, zc)
                g = cot_ref[0, :, x, :, zs].reshape(rows, zc).astype(F32)
                delta_ref[0, x, :, zs] = (g * (cumulative + t * density)).astype(BF16)


def weight_grad_kernel(planes_ref, delta_ref, out_ref, acc_ref, d_ref, bias_ref, *, yb):
    _, nx, rows, z = delta_ref.shape
    step = pl.program_id(0)

    @pl.when(step == 0)
    def _():
        acc_ref[...] = jnp.zeros_like(acc_ref)
        bias_ref[...] = jnp.zeros_like(bias_ref)

    nt = (((1,), (1,)), ((), ()))
    for q in range(nx // 2):
        for xo in range(2):
            v = delta_ref[0, 2 * q + xo]
            before, after = shifted(v)
            for k, part in enumerate((after, v, before)):
                d_ref[(k * 2 + xo) * rows:(k * 2 + xo + 1) * rows] = part
            bias_ref[...] += lax.dot_general(jnp.ones((8, z), BF16), v, nt, preferred_element_type=F32)
        a = planes_ref[0, 2 * q:2 * q + 4].reshape(4 * rows, z)
        acc_ref[...] += lax.dot_general(d_ref[...], a, nt, preferred_element_type=F32)

    @pl.when(step == pl.num_programs(0) - 1)
    def _():
        gather_rows = one_hot_cols(rows, yb, F32)
        gather_cols = one_hot_rows(rows, yb, F32)
        offset = band(rows, yb)
        exact = dict(preferred_element_type=F32, precision=lax.Precision.HIGHEST)
        for i in range(3):
            for k in range(3):
                t = jnp.zeros((rows, rows), F32)
                for xo in range(2):
                    r0 = (k * 2 + xo) * rows
                    c0 = (xo + i) * rows
                    t = t + acc_ref[r0:r0 + rows, c0:c0 + rows]
                for j in range(3):
                    masked = jnp.where(offset == j - 1, t, 0.0)
                    half = jnp.dot(masked, gather_cols, **exact)
                    out_ref[(i * 3 + j) * 3 + k] = jnp.dot(gather_rows, half, **exact)
        c = out_ref.shape[1]
        total = jnp.dot(bias_ref[...], gather_cols, **exact)
        out_ref[27] = jnp.broadcast_to(total[0:1], (c, c))


def input_grad_kernel(delta_ref, lo_ref, hi_ref, taps_ref, out_ref, w_ref, s_ref):
    _, nx, rows, z = delta_ref.shape
    _, c, _, yb, _ = out_ref.shape

    @pl.when(pl.program_id(0) == 0)
    def _():
        build_weights(taps_ref, w_ref, rows, yb, True)

    for p in range(nx + 2):
        if p == 0:
            v = lo_ref[0, 0]
        elif p == nx + 1:
            v = hi_ref[0, 0]
        else:
            v = delta_ref[0, p - 1]
        before, after = shifted(v)
        at = slice(p * rows, (p + 1) * rows)
        s_ref[0, at] = after
        s_ref[1, at] = v
        s_ref[2, at] = before
    zc = 256
    for q in range(nx // 2):
        at = slice(2 * q * rows, (2 * q + 4) * rows)
        for n in range(z // zc):
            zs = slice(n * zc, (n + 1) * zc)
            g = jnp.dot(w_ref[0], s_ref[0, at, zs], preferred_element_type=F32)
            g += jnp.dot(w_ref[1], s_ref[1, at, zs], preferred_element_type=F32)
            g += jnp.dot(w_ref[2], s_ref[2, at, zs], preferred_element_type=F32)
            for xo in range(2):
                part = g[xo * rows:(xo + 1) * rows].astype(BF16)
                out_ref[0, :, 2 * q + xo, :, zs] = part.reshape(c, yb, zc)


def native(c, nx, yb, z):
    return pl.BlockSpec((1, c, nx, yb, z), lambda b: (b, 0, 0, 0, 0))


def plain(nx, rows, z):
    return pl.BlockSpec((1, nx, rows, z), lambda b: (b, 0, 0, 0))


def whole(*shape):
    return pl.BlockSpec(shape, lambda b: (0,) * len(shape))


PARAMS = dict(vmem_limit_bytes=60 * 1024 * 1024, dimension_semantics=("arbitrary",))


def forward(activations, lo, hi, cotangent, taps, bias):
    nb, c, nx, yb, z = activations.shape
    rows = c * yb
    return pl.pallas_call(
        forward_kernel,
        grid=(nb,),
        in_specs=[native(c, nx, yb, z), native(c, 1, yb, z), native(c, 1, yb, z), native(c, nx, yb, z),
                  whole(27, c, c), whole(rows, 128)],
        out_specs=[native(c, nx, yb, z), plain(nx, rows, z), plain(nx + 2, rows, z)],
        out_shape=[jax.ShapeDtypeStruct((nb, c, nx, yb, z), BF16),
                   jax.ShapeDtypeStruct((nb, nx, rows, z), BF16),
                   jax.ShapeDtypeStruct((nb, nx + 2, rows, z), BF16)],
        scratch_shapes=[pltpu.VMEM((3, 2 * rows, 4 * rows), BF16),
                        pltpu.VMEM((3, (nx + 2) * rows, z), BF16)],
        compiler_params=pltpu.CompilerParams(**PARAMS),
        cost_estimate=pl.CostEstimate(flops=nb * nx * 3 * 256 * 512 * z, bytes_accessed=10 << 20, transcendentals=0),
        name="forward",
    )(activations, lo, hi, cotangent, taps, bias)


def weight_grad(planes, delta, c):
    nb, nx, rows, z = delta.shape
    yb = rows // c
    return pl.pallas_call(
        functools.partial(weight_grad_kernel, yb=yb),
        grid=(nb,),
        in_specs=[plain(nx + 2, rows, z), plain(nx, rows, z)],
        out_specs=whole(28, c, c),
        out_shape=jax.ShapeDtypeStruct((28, c, c), F32),
        scratch_shapes=[pltpu.VMEM((6 * rows, 4 * rows), F32),
                        pltpu.VMEM((6 * rows, z), BF16),
                        pltpu.VMEM((8, rows), F32)],
        compiler_params=pltpu.CompilerParams(**PARAMS),
        cost_estimate=pl.CostEstimate(flops=nb * nx * 3 * 256 * 512 * z, bytes_accessed=10 << 20, transcendentals=0),
        name="weight_grad",
    )(planes, delta)


def input_grad(delta, lo, hi, taps, c):
    nb, nx, rows, z = delta.shape
    yb = rows // c
    return pl.pallas_call(
        input_grad_kernel,
        grid=(nb,),
        in_specs=[plain(nx, rows, z), plain(1, rows, z), plain(1, rows, z), whole(27, c, c)],
        out_specs=native(c, nx, yb, z),
        out_shape=jax.ShapeDtypeStruct((nb, c, nx, yb, z), BF16),
        scratch_shapes=[pltpu.VMEM((3, 2 * rows, 4 * rows), BF16),
                        pltpu.VMEM((3, (nx + 2) * rows, z), BF16)],
        compiler_params=pltpu.CompilerParams(**PARAMS),
        cost_estimate=pl.CostEstimate(flops=nb * nx * 3 * 256 * 512 * z, bytes_accessed=10 << 20, transcendentals=0),
        name="input_grad",
    )(delta, lo, hi, taps)


def faces(block, dim):
    count = lax.axis_size("gx")
    up = [(i, i + 1) for i in range(count - 1)]
    down = [(t, s) for s, t in up]
    n = block.shape[dim]
    lo = lax.ppermute(lax.slice_in_dim(block, n - 1, n, axis=dim), "gx", up)
    hi = lax.ppermute(lax.slice_in_dim(block, 0, 1, axis=dim), "gx", down)
    return lo, hi


def per_device(activations, cotangent, kernel, channel_bias):
    nb, c, nx, yb, z = activations.shape
    rows = c * yb
    taps = jnp.transpose(kernel, (2, 3, 4, 0, 1)).reshape(27, c, c)
    taps_back = jnp.transpose(kernel, (2, 3, 4, 1, 0)).reshape(27, c, c)
    bias = jnp.broadcast_to(jnp.repeat(channel_bias, yb)[:, None], (rows, 128))
    lo, hi = faces(activations, 2)
    activated, delta, planes = forward(activations, lo, hi, cotangent, taps, bias)
    dlo, dhi = faces(delta, 1)
    sums = weight_grad(planes, delta, c)
    cells = nb * nx * yb * z * lax.axis_size("gx")
    reduced = lax.psum(sums, "gx") * (float(cells) ** -0.5)
    grad_input = input_grad(delta, dlo, dhi, taps_back, c)
    grad_kernel = jnp.transpose(reduced[:27].reshape(3, 3, 3, c, c), (3, 4, 0, 1, 2))
    return activated, grad_input, grad_kernel, reduced[27, 0]


def solution(mesh):
    placed = (P("grp", None, "gx", None, None), P("grp", None, "gx", None, None), P(), P())
    return jax.shard_map(
        per_device,
        mesh=mesh,
        in_specs=placed,
        out_specs=(
            P("grp", None, "gx", None, None),
            P("grp", None, "gx", None, None),
            P("grp", None, None, None, None),
            P("grp"),
        ),
        check_vma=False,
    )
```

```python
import functools

import jax
import jax.numpy as jnp
from jax import lax
from jax.experimental import pallas as pl
from jax.experimental.pallas import tpu as pltpu
from jax.sharding import PartitionSpec as P

F32 = jnp.float32
BF16 = jnp.bfloat16


def one_hot_rows(rows, group, dtype):
    r = lax.broadcasted_iota(jnp.int32, (rows, rows // group), 0)
    c = lax.broadcasted_iota(jnp.int32, (rows, rows // group), 1)
    return jnp.where(r // group == c, 1.0, 0.0).astype(dtype)


def one_hot_cols(rows, group, dtype):
    r = lax.broadcasted_iota(jnp.int32, (rows // group, rows), 0)
    c = lax.broadcasted_iota(jnp.int32, (rows // group, rows), 1)
    return jnp.where(c // group == r, 1.0, 0.0).astype(dtype)


def band(rows, yb):
    r = lax.broadcasted_iota(jnp.int32, (rows, rows), 0)
    c = lax.broadcasted_iota(jnp.int32, (rows, rows), 1)
    return c % yb - r % yb


def build_weights(taps_ref, w_ref, rows, yb, backward):
    spread_rows = one_hot_rows(rows, yb, BF16)
    spread_cols = one_hot_cols(rows, yb, BF16)
    offset = band(rows, yb)
    w_ref[...] = jnp.zeros_like(w_ref)
    for i in range(3):
        for k in range(3):
            block = jnp.zeros((rows, rows), F32)
            for j in range(3):
                tap = taps_ref[(i * 3 + j) * 3 + k]
                wide = jnp.dot(tap, spread_cols, preferred_element_type=F32).astype(BF16)
                full = jnp.dot(spread_rows, wide, preferred_element_type=F32)
                want = (1 - j) if backward else (j - 1)
                block = block + jnp.where(offset == want, full, 0.0)
            block = block.astype(BF16)
            for xo in range(2):
                xi = xo - i + 2 if backward else xo + i
                w_ref[k, xo * rows:(xo + 1) * rows, xi * rows:(xi + 1) * rows] = block


def shifted(v):
    zero = jnp.zeros((v.shape[0], 1), v.dtype)
    return (
        jnp.concatenate([zero, v[:, :-1]], axis=1),
        jnp.concatenate([v[:, 1:], zero], axis=1),
    )


def forward_kernel(act_ref, lo_ref, hi_ref, cot_ref, taps_ref, bias_ref,
                   activated_ref, delta_ref, planes_ref, w_ref, s_ref):
    _, c, nx, yb, z = act_ref.shape
    rows = c * yb

    @pl.when(pl.program_id(0) == 0)
    def _():
        build_weights(taps_ref, w_ref, rows, yb, False)

    for p in range(nx + 2):
        if p == 0:
            v = lo_ref[0, :, 0]
        elif p == nx + 1:
            v = hi_ref[0, :, 0]
        else:
            v = act_ref[0, :, p - 1]
        v = v.reshape(rows, z)
        planes_ref[0, p] = v
        before, after = shifted(v)
        at = slice(p * rows, (p + 1) * rows)
        s_ref[0, at] = before
        s_ref[1, at] = v
        s_ref[2, at] = after
    zc = 256
    for q in range(nx // 2):
        at = slice(2 * q * rows, (2 * q + 4) * rows)
        for n in range(z // zc):
            zs = slice(n * zc, (n + 1) * zc)
            pre = jnp.dot(w_ref[0], s_ref[0, at, zs], preferred_element_type=F32)
            pre += jnp.dot(w_ref[1], s_ref[1, at, zs], preferred_element_type=F32)
            pre += jnp.dot(w_ref[2], s_ref[2, at, zs], preferred_element_type=F32)
            for xo in range(2):
                x = 2 * q + xo
                t = pre[xo * rows:(xo + 1) * rows] + bias_ref[:, 0:1]
                cumulative = 0.5 * (1.0 + lax.erf(t * 0.7071067811865476))
                density = jnp.exp(-0.5 * t * t) * 0.3989422804014327
                activated_ref[0, :, x, :, zs] = (t * cumulative).astype(BF16).reshape(c, yb, zc)
                g = cot_ref[0, :, x, :, zs].reshape(rows, zc).astype(F32)
                delta_ref[0, x, :, zs] = (g * (cumulative + t * density)).astype(BF16)


def weight_grad_kernel(planes_ref, delta_ref, out_ref, acc_ref, d_ref, bias_ref, *, yb):
    _, nx, rows, z = delta_ref.shape
    step = pl.program_id(0)

    @pl.when(step == 0)
    def _():
        acc_ref[...] = jnp.zeros_like(acc_ref)
        bias_ref[...] = jnp.zeros_like(bias_ref)

    nt = (((1,), (1,)), ((), ()))
    for q in range(nx // 2):
        for xo in range(2):
            v = delta_ref[0, 2 * q + xo]
            before, after = shifted(v)
            for k, part in enumerate((after, v, before)):
                d_ref[(k * 2 + xo) * rows:(k * 2 + xo + 1) * rows] = part
            bias_ref[...] += lax.dot_general(jnp.ones((8, z), BF16), v, nt, preferred_element_type=F32)
        a = planes_ref[0, 2 * q:2 * q + 4].reshape(4 * rows, z)
        acc_ref[...] += lax.dot_general(d_ref[...], a, nt, preferred_element_type=F32)

    @pl.when(step == pl.num_programs(0) - 1)
    def _():
        c = rows // yb
        out_ref[...] = jnp.zeros_like(out_ref)

        def put(tap, value):
            row, col = tap // 4 * c, tap % 4 * c
            out_ref[row:row + c, col:col + c] = value

        gather_rows = one_hot_cols(rows, yb, F32)
        gather_cols = one_hot_rows(rows, yb, F32)
        offset = band(rows, yb)
        exact = dict(preferred_element_type=F32, precision=lax.Precision.HIGHEST)
        for i in range(3):
            for k in range(3):
                t = jnp.zeros((rows, rows), F32)
                for xo in range(2):
                    r0 = (k * 2 + xo) * rows
                    c0 = (xo + i) * rows
                    t = t + acc_ref[r0:r0 + rows, c0:c0 + rows]
                for j in range(3):
                    masked = jnp.where(offset == j - 1, t, 0.0)
                    half = jnp.dot(masked, gather_cols, **exact)
                    put((i * 3 + j) * 3 + k, jnp.dot(gather_rows, half, **exact))
        total = jnp.dot(bias_ref[...], gather_cols, **exact)
        put(27, jnp.broadcast_to(total[0:1], (c, c)))


def input_grad_kernel(delta_ref, lo_ref, hi_ref, taps_ref, out_ref, w_ref, s_ref):
    _, nx, rows, z = delta_ref.shape
    _, c, _, yb, _ = out_ref.shape

    @pl.when(pl.program_id(0) == 0)
    def _():
        build_weights(taps_ref, w_ref, rows, yb, True)

    for p in range(nx + 2):
        if p == 0:
            v = lo_ref[0, 0]
        elif p == nx + 1:
            v = hi_ref[0, 0]
        else:
            v = delta_ref[0, p - 1]
        before, after = shifted(v)
        at = slice(p * rows, (p + 1) * rows)
        s_ref[0, at] = after
        s_ref[1, at] = v
        s_ref[2, at] = before
    zc = 256
    for q in range(nx // 2):
        at = slice(2 * q * rows, (2 * q + 4) * rows)
        for n in range(z // zc):
            zs = slice(n * zc, (n + 1) * zc)
            g = jnp.dot(w_ref[0], s_ref[0, at, zs], preferred_element_type=F32)
            g += jnp.dot(w_ref[1], s_ref[1, at, zs], preferred_element_type=F32)
            g += jnp.dot(w_ref[2], s_ref[2, at, zs], preferred_element_type=F32)
            for xo in range(2):
                part = g[xo * rows:(xo + 1) * rows].astype(BF16)
                out_ref[0, :, 2 * q + xo, :, zs] = part.reshape(c, yb, zc)


def native(c, nx, yb, z):
    return pl.BlockSpec((1, c, nx, yb, z), lambda b: (b, 0, 0, 0, 0))


def plain(nx, rows, z):
    return pl.BlockSpec((1, nx, rows, z), lambda b: (b, 0, 0, 0))


def whole(*shape):
    return pl.BlockSpec(shape, lambda b: (0,) * len(shape))


PARAMS = dict(vmem_limit_bytes=60 * 1024 * 1024, dimension_semantics=("arbitrary",))


def forward(activations, lo, hi, cotangent, taps, bias):
    nb, c, nx, yb, z = activations.shape
    rows = c * yb
    return pl.pallas_call(
        forward_kernel,
        grid=(nb,),
        in_specs=[native(c, nx, yb, z), native(c, 1, yb, z), native(c, 1, yb, z), native(c, nx, yb, z),
                  whole(27, c, c), whole(rows, 128)],
        out_specs=[native(c, nx, yb, z), plain(nx, rows, z), plain(nx + 2, rows, z)],
        out_shape=[jax.ShapeDtypeStruct((nb, c, nx, yb, z), BF16),
                   jax.ShapeDtypeStruct((nb, nx, rows, z), BF16),
                   jax.ShapeDtypeStruct((nb, nx + 2, rows, z), BF16)],
        scratch_shapes=[pltpu.VMEM((3, 2 * rows, 4 * rows), BF16),
                        pltpu.VMEM((3, (nx + 2) * rows, z), BF16)],
        compiler_params=pltpu.CompilerParams(**PARAMS),
        cost_estimate=pl.CostEstimate(flops=nb * nx * 3 * 256 * 512 * z, bytes_accessed=10 << 20, transcendentals=0),
        name="forward",
    )(activations, lo, hi, cotangent, taps, bias)


def all_sum_kernel(x_ref, out_ref, recv, mine, gathered, send1, recv1, send2, recv2, *, n, scale):
    me = lax.axis_index("gx")
    c = out_ref.shape[1]

    def scatter(d, owner):
        return pltpu.make_async_remote_copy(
            src_ref=x_ref.at[owner], dst_ref=recv.at[d - 1], send_sem=send1.at[d - 1], recv_sem=recv1.at[d - 1],
            device_id={"gx": owner}, device_id_type=pl.DeviceIdType.MESH)

    def spread(d, slot, peer):
        return pltpu.make_async_remote_copy(
            src_ref=mine, dst_ref=gathered.at[slot], send_sem=send2.at[d - 1], recv_sem=recv2.at[d - 1],
            device_id={"gx": peer}, device_id_type=pl.DeviceIdType.MESH)

    def each(f):
        def step(d, carry):
            f(d, lax.rem(me + d, n), lax.rem(me + n - d, n))
            return carry
        lax.fori_loop(1, n, step, 0)

    barrier = pltpu.get_barrier_semaphore()
    each(lambda d, to, source: pl.semaphore_signal(
        barrier, inc=1, device_id={"gx": to}, device_id_type=pl.DeviceIdType.MESH))
    pl.semaphore_wait(barrier, n - 1)
    each(lambda d, to, source: scatter(d, to).start())
    each(lambda d, to, source: scatter(d, to).wait_recv())
    total = (x_ref[me] + jnp.sum(recv[...], axis=0)) * scale
    mine[...] = total
    gathered[me] = total
    each(lambda d, to, source: spread(d, me, to).start())
    each(lambda d, to, source: spread(d, source, to).wait_recv())
    flat = gathered[...].reshape(-1, 128)
    for tap in range(28):
        row, col = tap // 4 * c, tap % 4 * c
        out_ref[tap] = flat[row:row + c, col:col + c]
    each(lambda d, to, source: scatter(d, to).wait_send())
    each(lambda d, to, source: spread(d, me, to).wait_send())


def chunk_rows(c, n):
    rows = 28 * c * c // 128
    return -(-rows // (8 * n)) * 8


def all_sum(sums, c, n, scale):
    r = chunk_rows(c, n)
    vmem = pl.BlockSpec(memory_space=pltpu.VMEM)
    return pl.pallas_call(
        functools.partial(all_sum_kernel, n=n, scale=scale),
        in_specs=[vmem],
        out_specs=vmem,
        out_shape=jax.ShapeDtypeStruct((28, c, c), F32),
        scratch_shapes=[pltpu.VMEM((n - 1, r, 128), F32), pltpu.VMEM((r, 128), F32), pltpu.VMEM((n, r, 128), F32)]
        + [pltpu.SemaphoreType.DMA((n - 1,))] * 4,
        compiler_params=pltpu.CompilerParams(collective_id=0, has_side_effects=True),
        cost_estimate=pl.CostEstimate(flops=1 << 20, bytes_accessed=16 << 20, transcendentals=0),
        name="all_sum",
    )(sums.reshape(n, r, 128))


def weight_grad(planes, delta, c, n):
    nb, nx, rows, z = delta.shape
    yb = rows // c
    return pl.pallas_call(
        functools.partial(weight_grad_kernel, yb=yb),
        grid=(nb,),
        in_specs=[plain(nx + 2, rows, z), plain(nx, rows, z)],
        out_specs=whole(n * chunk_rows(c, n), 128),
        out_shape=jax.ShapeDtypeStruct((n * chunk_rows(c, n), 128), F32),
        scratch_shapes=[pltpu.VMEM((6 * rows, 4 * rows), F32),
                        pltpu.VMEM((6 * rows, z), BF16),
                        pltpu.VMEM((8, rows), F32)],
        compiler_params=pltpu.CompilerParams(**PARAMS),
        cost_estimate=pl.CostEstimate(flops=nb * nx * 3 * 256 * 512 * z, bytes_accessed=10 << 20, transcendentals=0),
        name="weight_grad",
    )(planes, delta)


def input_grad(delta, lo, hi, taps, c):
    nb, nx, rows, z = delta.shape
    yb = rows // c
    return pl.pallas_call(
        input_grad_kernel,
        grid=(nb,),
        in_specs=[plain(nx, rows, z), plain(1, rows, z), plain(1, rows, z), whole(27, c, c)],
        out_specs=native(c, nx, yb, z),
        out_shape=jax.ShapeDtypeStruct((nb, c, nx, yb, z), BF16),
        scratch_shapes=[pltpu.VMEM((3, 2 * rows, 4 * rows), BF16),
                        pltpu.VMEM((3, (nx + 2) * rows, z), BF16)],
        compiler_params=pltpu.CompilerParams(**PARAMS),
        cost_estimate=pl.CostEstimate(flops=nb * nx * 3 * 256 * 512 * z, bytes_accessed=10 << 20, transcendentals=0),
        name="input_grad",
    )(delta, lo, hi, taps)


def faces(block, dim):
    count = lax.axis_size("gx")
    up = [(i, i + 1) for i in range(count - 1)]
    down = [(t, s) for s, t in up]
    n = block.shape[dim]
    lo = lax.ppermute(lax.slice_in_dim(block, n - 1, n, axis=dim), "gx", up)
    hi = lax.ppermute(lax.slice_in_dim(block, 0, 1, axis=dim), "gx", down)
    return lo, hi


def per_device(activations, cotangent, kernel, channel_bias):
    nb, c, nx, yb, z = activations.shape
    rows = c * yb
    taps = jnp.transpose(kernel, (2, 3, 4, 0, 1)).reshape(27, c, c)
    taps_back = jnp.transpose(kernel, (2, 3, 4, 1, 0)).reshape(27, c, c)
    bias = jnp.broadcast_to(jnp.repeat(channel_bias, yb)[:, None], (rows, 128))
    lo, hi = faces(activations, 2)
    activated, delta, planes = forward(activations, lo, hi, cotangent, taps, bias)
    dlo, dhi = faces(delta, 1)
    n = lax.axis_size("gx")
    sums = weight_grad(planes, delta, c, n)
    cells = nb * nx * yb * z * n
    reduced = all_sum(sums, c, n, float(cells) ** -0.5)
    grad_input = input_grad(delta, dlo, dhi, taps_back, c)
    grad_kernel = jnp.transpose(reduced[:27].reshape(3, 3, 3, c, c), (3, 4, 0, 1, 2))
    return activated, grad_input, grad_kernel, reduced[27, 0]


def solution(mesh):
    placed = (P("grp", None, "gx", None, None), P("grp", None, "gx", None, None), P(), P())
    return jax.shard_map(
        per_device,
        mesh=mesh,
        in_specs=placed,
        out_specs=(
            P("grp", None, "gx", None, None),
            P("grp", None, "gx", None, None),
            P("grp", None, None, None, None),
            P("grp"),
        ),
        check_vma=False,
    )
```

```python
import functools

import jax
import jax.numpy as jnp
from jax import lax
from jax.experimental import pallas as pl
from jax.experimental.pallas import tpu as pltpu
from jax.sharding import PartitionSpec as P

F32 = jnp.float32
BF16 = jnp.bfloat16


def one_hot_rows(rows, group, dtype):
    r = lax.broadcasted_iota(jnp.int32, (rows, rows // group), 0)
    c = lax.broadcasted_iota(jnp.int32, (rows, rows // group), 1)
    return jnp.where(r // group == c, 1.0, 0.0).astype(dtype)


def one_hot_cols(rows, group, dtype):
    r = lax.broadcasted_iota(jnp.int32, (rows // group, rows), 0)
    c = lax.broadcasted_iota(jnp.int32, (rows // group, rows), 1)
    return jnp.where(c // group == r, 1.0, 0.0).astype(dtype)


def band(rows, yb):
    r = lax.broadcasted_iota(jnp.int32, (rows, rows), 0)
    c = lax.broadcasted_iota(jnp.int32, (rows, rows), 1)
    return c % yb - r % yb


def build_weights(taps_ref, w_ref, rows, yb, backward):
    spread_rows = one_hot_rows(rows, yb, BF16)
    spread_cols = one_hot_cols(rows, yb, BF16)
    offset = band(rows, yb)
    w_ref[...] = jnp.zeros_like(w_ref)
    for i in range(3):
        for k in range(3):
            block = jnp.zeros((rows, rows), F32)
            for j in range(3):
                tap = taps_ref[(i * 3 + j) * 3 + k]
                wide = jnp.dot(tap, spread_cols, preferred_element_type=F32).astype(BF16)
                full = jnp.dot(spread_rows, wide, preferred_element_type=F32)
                want = (1 - j) if backward else (j - 1)
                block = block + jnp.where(offset == want, full, 0.0)
            block = block.astype(BF16)
            for xo in range(2):
                xi = xo - i + 2 if backward else xo + i
                w_ref[k, xo * rows:(xo + 1) * rows, xi * rows:(xi + 1) * rows] = block


def weights_kernel(taps_ref, taps_back_ref, bias_ref, w_ref, w_back_ref, column_ref, *, yb):
    rows = w_ref.shape[1] // 2
    column = jnp.sum(one_hot_rows(rows, yb, F32) * bias_ref[...], axis=1, keepdims=True)
    column_ref[...] = jnp.broadcast_to(column, column_ref.shape)
    build_weights(taps_ref, w_ref, rows, yb, False)
    build_weights(taps_back_ref, w_back_ref, rows, yb, True)


def shifted(v):
    zero = jnp.zeros((v.shape[0], 1), v.dtype)
    return (
        jnp.concatenate([zero, v[:, :-1]], axis=1),
        jnp.concatenate([v[:, 1:], zero], axis=1),
    )


def forward_kernel(act_ref, lo_ref, hi_ref, cot_ref, w_ref, bias_ref,
                   activated_ref, delta_ref, planes_ref, s_ref):
    _, c, nx, yb, z = act_ref.shape
    rows = c * yb
    for p in range(nx + 2):
        if p == 0:
            v = lo_ref[0, :, 0]
        elif p == nx + 1:
            v = hi_ref[0, :, 0]
        else:
            v = act_ref[0, :, p - 1]
        v = v.reshape(rows, z)
        planes_ref[0, p] = v
        before, after = shifted(v)
        at = slice(p * rows, (p + 1) * rows)
        s_ref[0, at] = before
        s_ref[1, at] = v
        s_ref[2, at] = after
    zc = 256
    for q in range(nx // 2):
        at = slice(2 * q * rows, (2 * q + 4) * rows)
        for n in range(z // zc):
            zs = slice(n * zc, (n + 1) * zc)
            pre = jnp.dot(w_ref[0], s_ref[0, at, zs], preferred_element_type=F32)
            pre += jnp.dot(w_ref[1], s_ref[1, at, zs], preferred_element_type=F32)
            pre += jnp.dot(w_ref[2], s_ref[2, at, zs], preferred_element_type=F32)
            for xo in range(2):
                x = 2 * q + xo
                t = pre[xo * rows:(xo + 1) * rows] + bias_ref[:, 0:1]
                cumulative = 0.5 * (1.0 + lax.erf(t * 0.7071067811865476))
                density = jnp.exp(-0.5 * t * t) * 0.3989422804014327
                activated_ref[0, :, x, :, zs] = (t * cumulative).astype(BF16).reshape(c, yb, zc)
                g = cot_ref[0, :, x, :, zs].reshape(rows, zc).astype(F32)
                delta_ref[0, x, :, zs] = (g * (cumulative + t * density)).astype(BF16)


def weight_grad_kernel(planes_ref, delta_ref, out_ref, acc_ref, d_ref, bias_ref, *, yb):
    _, nx, rows, z = delta_ref.shape
    step = pl.program_id(0)

    @pl.when(step == 0)
    def _():
        acc_ref[...] = jnp.zeros_like(acc_ref)
        bias_ref[...] = jnp.zeros_like(bias_ref)

    nt = (((1,), (1,)), ((), ()))
    for q in range(nx // 2):
        for xo in range(2):
            v = delta_ref[0, 2 * q + xo]
            before, after = shifted(v)
            for k, part in enumerate((after, v, before)):
                d_ref[(k * 2 + xo) * rows:(k * 2 + xo + 1) * rows] = part
            bias_ref[...] += lax.dot_general(jnp.ones((8, z), BF16), v, nt, preferred_element_type=F32)
        a = planes_ref[0, 2 * q:2 * q + 4].reshape(4 * rows, z)
        acc_ref[...] += lax.dot_general(d_ref[...], a, nt, preferred_element_type=F32)

    @pl.when(step == pl.num_programs(0) - 1)
    def _():
        c = rows // yb
        out_ref[...] = jnp.zeros_like(out_ref)

        def put(tap, value):
            row, col = tap // 4 * c, tap % 4 * c
            out_ref[row:row + c, col:col + c] = value

        gather_rows = one_hot_cols(rows, yb, F32)
        gather_cols = one_hot_rows(rows, yb, F32)
        offset = band(rows, yb)
        exact = dict(preferred_element_type=F32, precision=lax.Precision.HIGHEST)
        for i in range(3):
            for k in range(3):
                t = jnp.zeros((rows, rows), F32)
                for xo in range(2):
                    r0 = (k * 2 + xo) * rows
                    c0 = (xo + i) * rows
                    t = t + acc_ref[r0:r0 + rows, c0:c0 + rows]
                for j in range(3):
                    masked = jnp.where(offset == j - 1, t, 0.0)
                    half = jnp.dot(masked, gather_cols, **exact)
                    put((i * 3 + j) * 3 + k, jnp.dot(gather_rows, half, **exact))
        total = jnp.dot(bias_ref[...], gather_cols, **exact)
        put(27, jnp.broadcast_to(total[0:1], (c, c)))


def input_grad_kernel(delta_ref, lo_ref, hi_ref, w_ref, out_ref, s_ref):
    _, nx, rows, z = delta_ref.shape
    _, c, _, yb, _ = out_ref.shape
    for p in range(nx + 2):
        if p == 0:
            v = lo_ref[0, 0]
        elif p == nx + 1:
            v = hi_ref[0, 0]
        else:
            v = delta_ref[0, p - 1]
        before, after = shifted(v)
        at = slice(p * rows, (p + 1) * rows)
        s_ref[0, at] = after
        s_ref[1, at] = v
        s_ref[2, at] = before
    zc = 256
    for q in range(nx // 2):
        at = slice(2 * q * rows, (2 * q + 4) * rows)
        for n in range(z // zc):
            zs = slice(n * zc, (n + 1) * zc)
            g = jnp.dot(w_ref[0], s_ref[0, at, zs], preferred_element_type=F32)
            g += jnp.dot(w_ref[1], s_ref[1, at, zs], preferred_element_type=F32)
            g += jnp.dot(w_ref[2], s_ref[2, at, zs], preferred_element_type=F32)
            for xo in range(2):
                part = g[xo * rows:(xo + 1) * rows].astype(BF16)
                out_ref[0, :, 2 * q + xo, :, zs] = part.reshape(c, yb, zc)


def native(c, nx, yb, z):
    return pl.BlockSpec((1, c, nx, yb, z), lambda b: (b, 0, 0, 0, 0))


def plain(nx, rows, z):
    return pl.BlockSpec((1, nx, rows, z), lambda b: (b, 0, 0, 0))


def whole(*shape):
    return pl.BlockSpec(shape, lambda b: (0,) * len(shape))


PARAMS = dict(vmem_limit_bytes=60 * 1024 * 1024, dimension_semantics=("arbitrary",))


def weights(taps, taps_back, channel_bias, c, yb):
    rows = c * yb
    wide = jax.ShapeDtypeStruct((3, 2 * rows, 4 * rows), BF16)
    return pl.pallas_call(
        functools.partial(weights_kernel, yb=yb),
        out_shape=[wide, wide, jax.ShapeDtypeStruct((rows, 128), F32)],
        cost_estimate=pl.CostEstimate(flops=1 << 30, bytes_accessed=4 << 20, transcendentals=0),
        name="weights",
    )(taps, taps_back, channel_bias.reshape(1, c))


def forward(activations, lo, hi, cotangent, w, bias):
    nb, c, nx, yb, z = activations.shape
    rows = c * yb
    return pl.pallas_call(
        forward_kernel,
        grid=(nb,),
        in_specs=[native(c, nx, yb, z), native(c, 1, yb, z), native(c, 1, yb, z), native(c, nx, yb, z),
                  whole(3, 2 * rows, 4 * rows), whole(rows, 128)],
        out_specs=[native(c, nx, yb, z), plain(nx, rows, z), plain(nx + 2, rows, z)],
        out_shape=[jax.ShapeDtypeStruct((nb, c, nx, yb, z), BF16),
                   jax.ShapeDtypeStruct((nb, nx, rows, z), BF16),
                   jax.ShapeDtypeStruct((nb, nx + 2, rows, z), BF16)],
        scratch_shapes=[pltpu.VMEM((3, (nx + 2) * rows, z), BF16)],
        compiler_params=pltpu.CompilerParams(**PARAMS),
        cost_estimate=pl.CostEstimate(flops=nb * nx * 3 * 256 * 512 * z, bytes_accessed=10 << 20, transcendentals=0),
        name="forward",
    )(activations, lo, hi, cotangent, w, bias)


def all_sum_kernel(x_ref, out_ref, bias_ref, recv, mine, gathered, send1, recv1, send2, recv2, *, n, scale):
    me = lax.axis_index("gx")
    c = out_ref.shape[1]

    def scatter(d, owner):
        return pltpu.make_async_remote_copy(
            src_ref=x_ref.at[owner], dst_ref=recv.at[d - 1], send_sem=send1.at[d - 1], recv_sem=recv1.at[d - 1],
            device_id={"gx": owner}, device_id_type=pl.DeviceIdType.MESH)

    def spread(d, slot, peer):
        return pltpu.make_async_remote_copy(
            src_ref=mine, dst_ref=gathered.at[slot], send_sem=send2.at[d - 1], recv_sem=recv2.at[d - 1],
            device_id={"gx": peer}, device_id_type=pl.DeviceIdType.MESH)

    def each(f):
        def step(d, carry):
            f(d, lax.rem(me + d, n), lax.rem(me + n - d, n))
            return carry
        lax.fori_loop(1, n, step, 0)

    barrier = pltpu.get_barrier_semaphore()
    each(lambda d, to, source: pl.semaphore_signal(
        barrier, inc=1, device_id={"gx": to}, device_id_type=pl.DeviceIdType.MESH))
    pl.semaphore_wait(barrier, n - 1)
    each(lambda d, to, source: scatter(d, to).start())
    each(lambda d, to, source: scatter(d, to).wait_recv())
    total = (x_ref[me] + jnp.sum(recv[...], axis=0)) * scale
    mine[...] = total
    gathered[me] = total
    each(lambda d, to, source: spread(d, me, to).start())
    each(lambda d, to, source: spread(d, source, to).wait_recv())
    flat = gathered[...].reshape(-1, 128)
    for tap in range(27):
        row, col = tap // 4 * c, tap % 4 * c
        out_ref[tap] = flat[row:row + c, col:col + c]
    row, col = 27 // 4 * c, 27 % 4 * c
    bias_ref[...] = flat[row:row + 1, col:col + c]
    each(lambda d, to, source: scatter(d, to).wait_send())
    each(lambda d, to, source: spread(d, me, to).wait_send())


def chunk_rows(c, n):
    rows = 28 * c * c // 128
    return -(-rows // (8 * n)) * 8


def all_sum(sums, c, n, scale):
    r = chunk_rows(c, n)
    vmem = pl.BlockSpec(memory_space=pltpu.VMEM)
    return pl.pallas_call(
        functools.partial(all_sum_kernel, n=n, scale=scale),
        in_specs=[vmem],
        out_specs=[vmem, vmem],
        out_shape=[jax.ShapeDtypeStruct((27, c, c), F32), jax.ShapeDtypeStruct((1, c), F32)],
        scratch_shapes=[pltpu.VMEM((n - 1, r, 128), F32), pltpu.VMEM((r, 128), F32), pltpu.VMEM((n, r, 128), F32)]
        + [pltpu.SemaphoreType.DMA((n - 1,))] * 4,
        compiler_params=pltpu.CompilerParams(collective_id=0, has_side_effects=True),
        cost_estimate=pl.CostEstimate(flops=1 << 20, bytes_accessed=16 << 20, transcendentals=0),
        name="all_sum",
    )(sums.reshape(n, r, 128))


def weight_grad(planes, delta, c, n):
    nb, nx, rows, z = delta.shape
    yb = rows // c
    return pl.pallas_call(
        functools.partial(weight_grad_kernel, yb=yb),
        grid=(nb,),
        in_specs=[plain(nx + 2, rows, z), plain(nx, rows, z)],
        out_specs=whole(n * chunk_rows(c, n), 128),
        out_shape=jax.ShapeDtypeStruct((n * chunk_rows(c, n), 128), F32),
        scratch_shapes=[pltpu.VMEM((6 * rows, 4 * rows), F32),
                        pltpu.VMEM((6 * rows, z), BF16),
                        pltpu.VMEM((8, rows), F32)],
        compiler_params=pltpu.CompilerParams(**PARAMS),
        cost_estimate=pl.CostEstimate(flops=nb * nx * 3 * 256 * 512 * z, bytes_accessed=10 << 20, transcendentals=0),
        name="weight_grad",
    )(planes, delta)


def input_grad(delta, lo, hi, w, c):
    nb, nx, rows, z = delta.shape
    yb = rows // c
    return pl.pallas_call(
        input_grad_kernel,
        grid=(nb,),
        in_specs=[plain(nx, rows, z), plain(1, rows, z), plain(1, rows, z), whole(3, 2 * rows, 4 * rows)],
        out_specs=native(c, nx, yb, z),
        out_shape=jax.ShapeDtypeStruct((nb, c, nx, yb, z), BF16),
        scratch_shapes=[pltpu.VMEM((3, (nx + 2) * rows, z), BF16)],
        compiler_params=pltpu.CompilerParams(**PARAMS),
        cost_estimate=pl.CostEstimate(flops=nb * nx * 3 * 256 * 512 * z, bytes_accessed=10 << 20, transcendentals=0),
        name="input_grad",
    )(delta, lo, hi, w)


def faces(block, dim):
    count = lax.axis_size("gx")
    up = [(i, i + 1) for i in range(count - 1)]
    down = [(t, s) for s, t in up]
    n = block.shape[dim]
    lo = lax.ppermute(lax.slice_in_dim(block, n - 1, n, axis=dim), "gx", up)
    hi = lax.ppermute(lax.slice_in_dim(block, 0, 1, axis=dim), "gx", down)
    return lo, hi


def per_device(activations, cotangent, kernel, channel_bias):
    nb, c, nx, yb, z = activations.shape
    taps = jnp.transpose(kernel, (2, 3, 4, 0, 1)).reshape(27, c, c)
    taps_back = jnp.transpose(kernel, (2, 3, 4, 1, 0)).reshape(27, c, c)
    lo, hi = faces(activations, 2)
    w, w_back, column = weights(taps, taps_back, channel_bias, c, yb)
    activated, delta, planes = forward(activations, lo, hi, cotangent, w, column)
    dlo, dhi = faces(delta, 1)
    n = lax.axis_size("gx")
    sums = weight_grad(planes, delta, c, n)
    cells = nb * nx * yb * z * n
    kernel_sums, bias_sums = all_sum(sums, c, n, float(cells) ** -0.5)
    grad_input = input_grad(delta, dlo, dhi, w_back, c)
    grad_kernel = jnp.transpose(kernel_sums.reshape(3, 3, 3, c, c), (3, 4, 0, 1, 2))
    return activated, grad_input, grad_kernel, bias_sums.reshape(c)


def solution(mesh):
    placed = (P("grp", None, "gx", None, None), P("grp", None, "gx", None, None), P(), P())
    return jax.shard_map(
        per_device,
        mesh=mesh,
        in_specs=placed,
        out_specs=(
            P("grp", None, "gx", None, None),
            P("grp", None, "gx", None, None),
            P("grp", None, None, None, None),
            P("grp"),
        ),
        check_vma=False,
    )
```
